32 devices in a mesh: prod: 8 (over y, x, core), trip: 4 (over z).
Axes of the slice: x: 2, y: 2, z: 4, core: 2. Of those that a mesh axis runs over, the one named last changes fastest.
Arguments:
- trip_vecs: bfloat16 [65536, 128], P(('prod', 'trip'))
- table: bfloat16 [65536, 128], P('prod'), may hold values from -0.5 to 0.5
- consider: int32 [128, 4], P(('prod', 'trip')), may hold values from 0 to 127, as said below
- lengths: int32 [128, 4], P(('prod', 'trip')), may hold values from 1 to 512, as said below
- chosen: int32 [65536], P(('prod', 'trip')), may hold values from 0 to 2047, as said below
Outputs:
- losses: float32 [65536], P(('prod', 'trip'))
- trip_grads: float32 [65536, 128], P(('prod', 'trip'))
- table_grads: float32 [65536, 128], P('prod')
The draws below stay inside these ranges and needn't reach their ends.
Inputs may be any that keep to these rules, and one draw needn't show every extreme that they name: `consider`: each row names 4 different product blocks; the blocks named by the rows of one device are all different; at most 4 of them lie among the 16 blocks of one index of prod, and in every draw one index of prod gets exactly 4 from every device. `lengths`: every device has a row with 512 in its first and last column. chosen[t] = k * 512 + o with o < lengths[b, k] for the trip's block b.
All inputs are finite; a program needn't handle non-finite values.
Results may differ from the reference program's by a relative error of at most 0.0034.
Values may be sent and summed in bfloat16 or wider, within the bound.
No kernel may reach another device: no remote copies, remote signals or barrier semaphores. Data moves between devices by JAX's collectives and lax.ppermute only.
A program may use at most 192 MiB of HBM per device.

```python
import jax
import jax.numpy as jnp
from jax import lax

D = 128
BLOCK = 512
TRIP_ROWS = 512
K = 4
BLK_DEV = 16
TB_DEV = 4
PRODUCTS = 65536
TRIP_BLOCKS = 128
TRIPS = 65536
CAP = 4
N_PROD = 8
N_TRIP = 4


def draw_trip_vecs(key, part):
    values = jax.random.normal(jax.random.fold_in(key, 4), (TRIPS, D), jnp.float32)
    return jnp.clip(values, -6.0, 6.0).astype(jnp.bfloat16)


def draw_consider(key, part):
    busy_owner = jax.random.randint(jax.random.fold_in(key, 11), (), 0, N_PROD)
    request_count = TB_DEV * K

    def one_device(device):
        device_key = jax.random.fold_in(key, device + 1000)
        others = jax.random.permutation(jax.random.fold_in(device_key, 1), N_PROD - 1)
        others = (busy_owner + 1 + others) % N_PROD
        positions = jnp.arange(request_count)
        remainder = jnp.maximum(positions - CAP, 0)
        owners = jnp.where(positions < CAP, busy_owner, others[remainder % (N_PROD - 1)])
        ranks = jnp.where(positions < CAP, positions, remainder // (N_PROD - 1))

        def owner_perm(owner_index):
            return jax.random.permutation(jax.random.fold_in(device_key, owner_index + 7), BLK_DEV)
        local_perm = jax.vmap(owner_perm)(jnp.arange(N_PROD))
        within = local_perm[owners, ranks]
        block_ids = owners * BLK_DEV + within
        shuffle = jax.random.permutation(jax.random.fold_in(device_key, 3), request_count)
        return block_ids[shuffle].reshape(TB_DEV, K)
    return jax.vmap(one_device)(jnp.arange(N_PROD * N_TRIP)).reshape(TRIP_BLOCKS, K).astype(jnp.int32)


def lengths_and_choices(key):
    base_key = jax.random.fold_in(key, 77)
    block_lengths = jax.random.randint(jax.random.fold_in(base_key, 1), (TRIP_BLOCKS, K), 1, BLOCK + 1)
    leading = (jnp.arange(TRIP_BLOCKS) % TB_DEV == 0)[:, None]
    edge_cols = (jnp.arange(K) == 0) | (jnp.arange(K) == K - 1)
    block_lengths = jnp.where(leading & edge_cols[None, :], BLOCK, block_lengths)
    picks = jax.random.randint(jax.random.fold_in(base_key, 2), (TRIP_BLOCKS, TRIP_ROWS), 0, K)
    random_bits = jax.random.randint(jax.random.fold_in(base_key, 3), (TRIP_BLOCKS, TRIP_ROWS), 0, 1 << 20)
    limits = jnp.take_along_axis(block_lengths, picks, axis=1)
    choices = picks * BLOCK + random_bits % limits
    row_index = jnp.arange(TRIP_ROWS)[None, :]
    choices = jnp.where(leading & (row_index == 0), K * BLOCK - 1, choices)
    choices = jnp.where(leading & (row_index == 1), 0, choices)
    return (block_lengths.astype(jnp.int32), choices.reshape(TRIPS).astype(jnp.int32))


def draw_lengths(key, part):
    return lengths_and_choices(key)[0]


def draw_chosen(key, part):
    return lengths_and_choices(key)[1]


def block_levels(own_key, dims, split, low, largest):
    def one(axis_at, blocks):
        heights = jax.random.uniform(jax.random.fold_in(jax.random.fold_in(own_key, 6), axis_at), (blocks,), jnp.float32, low / len(split), largest / len(split))
        return jnp.repeat(jnp.exp(heights), dims[axis_at] // blocks).reshape((-1,) + (1,) * (len(dims) - axis_at - 1))

    gain = one(*split[0])
    for cut in split[1:]:
        gain = gain * one(*cut)
    return gain


def bell_draw(own_key, extent, scale, reach, cuts=(), dtype=jnp.bfloat16):
    result = scale * jax.random.normal(own_key, extent, jnp.float32)
    if cuts:
        result = result * block_levels(own_key, extent, cuts, -0.22, 0.18)
    return jnp.clip(result, -reach, reach).astype(dtype)


def setup_inputs(seed: int = 0) -> dict:
    streams_of = jax.random.split(jax.random.key(seed), 6)
    trip_vecs = draw_trip_vecs(jax.random.fold_in(streams_of[5], 71), 0)
    table = bell_draw(streams_of[1], (PRODUCTS, D), D ** -0.5, 0.5, ((0, 8),))
    consider = draw_consider(jax.random.fold_in(streams_of[5], 71), 0)
    lengths = draw_lengths(jax.random.fold_in(streams_of[5], 71), 0)
    chosen = draw_chosen(jax.random.fold_in(streams_of[5], 71), 0)
    return dict(trip_vecs=trip_vecs, table=table, consider=consider, lengths=lengths, chosen=chosen)


masked_fill = -1e30


def tile_terms(queries, panel, usable, chosen_pos):
    scores = lax.dot_general(queries, panel, (((1,), (1,)), ((), ())), preferred_element_type=jnp.float32)
    filled = jnp.where(usable[None, :], scores, masked_fill)
    peaks = jnp.max(filled, axis=1, keepdims=True)
    log_total = peaks[:, 0] + jnp.log(jnp.sum(jnp.exp(filled - peaks), axis=1))
    is_chosen = jnp.arange(scores.shape[1]).astype(jnp.int32)[None, :] == chosen_pos[:, None]
    picked_score = jnp.sum(jnp.where(is_chosen, scores, 0.0), axis=1)
    softmax_w = jnp.exp(filled - log_total[:, None])
    weights_grad = (softmax_w - is_chosen.astype(jnp.float32)).astype(jnp.bfloat16)
    trip_grad = jnp.dot(weights_grad, panel, preferred_element_type=jnp.float32)
    panel_grad = lax.dot_general(weights_grad, queries, (((0,), (0,)), ((), ())), preferred_element_type=jnp.float32)
    return log_total - picked_score, trip_grad, panel_grad.astype(jnp.bfloat16)


def reference(trip_vecs, table, consider, lengths, chosen):
    feature_dim = table.shape[1]
    block_count = table.shape[0] // BLOCK
    blocks = table.reshape(block_count, BLOCK, feature_dim)
    trip_blocks = consider.shape[0]
    trip_alpha = trip_vecs.reshape(trip_blocks, TRIP_ROWS, feature_dim)
    chosen_pos = chosen.reshape(trip_blocks, TRIP_ROWS)
    offsets = jnp.arange(BLOCK).astype(jnp.int32)

    def advance_block(totals, inputs):
        queries, block_ids, block_lengths, picks = inputs
        panel = blocks[block_ids].reshape(K * BLOCK, feature_dim)
        usable = (offsets[None, :] < block_lengths[:, None]).reshape(K * BLOCK)
        losses, trip_grad, panel_grad = tile_terms(queries, panel, usable, picks)
        totals = totals.at[block_ids].add(panel_grad.reshape(K, BLOCK, feature_dim).astype(jnp.float32))
        return totals, (losses, trip_grad)

    start = jnp.zeros((block_count, BLOCK, feature_dim), jnp.float32)
    totals, (losses, trip_grads) = lax.scan(advance_block, start, (trip_alpha, consider, lengths, chosen_pos))
    return losses.reshape(-1), trip_grads.reshape(-1, feature_dim), totals.reshape(-1, feature_dim)
```

```python
import functools

import jax
import jax.numpy as jnp
from jax import lax
from jax.experimental import pallas as pl
from jax.experimental.pallas import tpu as pltpu
from jax.sharding import PartitionSpec as P

BLOCK = 512
LANES = 128
NEG = -1e30
CHUNKS = 4
HEIGHTS = (256, 512)
LEN_BITS = 10
DIGIT = 128


f32, bf16, i32 = jnp.float32, jnp.bfloat16, jnp.int32
VMEM = pl.BlockSpec(memory_space=pltpu.VMEM)
SMEM = pl.BlockSpec(memory_space=pltpu.SMEM)


def by_height(length, body):
    low = 0
    for height in HEIGHTS:
        pl.when((length > low) & (length <= height))(functools.partial(body, height))
        low = height


def masked_scores(panel, queries, length):
    scores = lax.dot_general(panel, queries, (((1,), (1,)), ((), ())), preferred_element_type=f32)
    rows = lax.broadcasted_iota(i32, scores.shape, 0)
    return jnp.where(rows < length, scores, NEG), rows


def pair_weights(panel, queries, length, lse, picks):
    scores, rows = masked_scores(panel, queries, length)
    weights = jnp.exp(scores - lse)
    return jnp.where(rows == picks, weights - 1.0, weights).astype(bf16)


class Plane:
    def __init__(self, refs, dims):
        self.refs = refs
        self.tb, self.per_block, self.trips = dims
        self.here = self.tb * self.trips
        self.lines = (refs[0].shape[0] - self.here) // 2

    def numbers(self, out_ref):
        for j, ref in enumerate(self.refs):
            meta = ref[pl.ds(self.here, 2 * self.lines), :].astype(f32)
            meta = meta[: self.lines] * DIGIT + meta[self.lines :]
            out_ref[pl.ds(j * self.lines, self.lines), :] = meta.astype(i32)

    def chosen(self, out_ref, t):
        j = t // self.tb
        lanes = self.trips // LANES
        at = j * self.lines + 2 * self.tb + (t - j * self.tb) * lanes
        return jnp.concatenate([out_ref[pl.ds(at + i, 1), :] for i in range(lanes)], axis=1)

    def queries(self, out_ref, t):
        for j, ref in enumerate(self.refs):

            @pl.when((t >= j * self.tb) & (t < (j + 1) * self.tb))
            def _(j=j, ref=ref):
                at = pl.multiple_of((t - j * self.tb) * self.trips, self.trips)
                out_ref[...] = ref[pl.ds(at, self.trips), :]


def local_block(ident, odd, blocks):
    other = jnp.where(ident < blocks, ident + blocks, ident - blocks)
    return jnp.where(odd == 1, other, ident)


def load_panel(out_ref, tables, block, blocks):
    for half, ref in enumerate(tables):

        @pl.when((block >= half * blocks) & (block < (half + 1) * blocks))
        def _(half=half, ref=ref):
            at = pl.multiple_of((block - half * blocks) * BLOCK, BLOCK)
            out_ref[...] = ref[pl.ds(at, BLOCK), :]


def visit(place_ref, facts_ref, blocks, plane, before, pair, after):
    tb, per_block = plane.tb, plane.per_block

    def one_block(t, _):
        before(t)
        j = t // tb

        def one_entry(k, _):
            ident = facts_ref[j, t - j * tb, k] - place_ref[0]
            size = facts_ref[j, tb + t - j * tb, k]
            held = (ident >= 0) & (ident < 2 * blocks)
            pl.when(held)(lambda: pair(t, k, local_block(ident, place_ref[1], blocks), size))
            return 0

        lax.fori_loop(0, per_block, one_entry, 0)
        after(t)
        return 0

    lax.fori_loop(0, len(plane.refs) * tb, one_block, 0)


def lse_kernel(dims, start, place_ref, facts_ref, own_ref, side_ref, *refs):
    plane = Plane(refs[:-10], dims)
    lse_ref, picked_ref, codes_ref, counts_ref, query_ref, panel_ref, meta_ref, peak_ref, total_ref, pick_ref = refs[-10:]
    blocks = own_ref.shape[0] // BLOCK
    plane.numbers(meta_ref)
    for c in range(CHUNKS):
        counts_ref[c] = 0

    def before(t):
        plane.queries(query_ref, t)
        peak_ref[...] = jnp.full_like(peak_ref, NEG)
        total_ref[...] = jnp.zeros_like(total_ref)
        pick_ref[...] = jnp.zeros_like(pick_ref)

    def pair(t, k, block, length):
        within = jnp.where(block >= blocks, block - blocks, block)
        chunk = within // (blocks // CHUNKS)
        count = counts_ref[chunk]
        entry = (start + t) * plane.per_block + k
        codes_ref[chunk, count] = ((entry * 2 * blocks + block) << LEN_BITS) + length
        counts_ref[chunk] = count + 1
        load_panel(panel_ref, (own_ref, side_ref), block, blocks)
        picks = plane.chosen(meta_ref, t) - k * BLOCK

        def body(height):
            scores, rows = masked_scores(panel_ref[pl.ds(0, height), :], query_ref[...], length)
            peak = peak_ref[...]
            new = jnp.maximum(peak, jnp.max(scores, axis=0, keepdims=True))
            part = jnp.sum(jnp.exp(scores - new), axis=0, keepdims=True)
            total_ref[...] = total_ref[...] * jnp.exp(peak - new) + part
            peak_ref[...] = new
            pick_ref[...] += jnp.sum(jnp.where(rows == picks, scores, 0.0), axis=0, keepdims=True)

        by_height(length, body)

    def after(t):
        total = total_ref[...]
        lse_ref[pl.ds(t, 1), :] = peak_ref[...] + jnp.log(jnp.where(total > 0, total, 1.0))
        picked_ref[pl.ds(t, 1), :] = pick_ref[...]

    visit(place_ref, facts_ref, blocks, plane, before, pair, after)


def table_kernel(dims, chunk, groups, *refs):
    counts, codes, refs = refs[:groups], refs[groups : 2 * groups], refs[2 * groups :]
    own_ref, side_ref, lse_ref, refs = refs[0], refs[1], refs[2], refs[3:]
    plane = Plane(refs[:-6], dims)
    out_ref, wire_ref, query_ref, panel_ref, meta_ref, acc_ref = refs[-6:]
    blocks = own_ref.shape[0] // BLOCK
    here = out_ref.shape[0]
    plane.numbers(meta_ref)
    acc_ref[...] = jnp.zeros_like(acc_ref)

    def one_pair(i, last, code_ref):
        code = code_ref[chunk, i]
        length = code & ((1 << LEN_BITS) - 1)
        rest = code >> LEN_BITS
        entry = rest // (2 * blocks)
        block = rest - entry * 2 * blocks
        t = entry // plane.per_block
        pl.when(t != last)(lambda: plane.queries(query_ref, t))
        load_panel(panel_ref, (own_ref, side_ref), block, blocks)
        picks = plane.chosen(meta_ref, t) - (entry - t * plane.per_block) * BLOCK
        lse = lse_ref[pl.ds(t, 1), :]
        to = jnp.where(block >= blocks, block - blocks + here, block) - chunk * here

        def body(height):
            queries = query_ref[...]
            weights = pair_weights(panel_ref[pl.ds(0, height), :], queries, length, lse, picks)
            grad = jnp.dot(weights, queries, preferred_element_type=f32)
            acc_ref[to, pl.ds(0, height), :] += grad.astype(bf16).astype(f32)

        by_height(length, body)
        return t

    last = jnp.int32(-1)
    for count_ref, code_ref in zip(counts, codes):
        last = lax.fori_loop(0, count_ref[chunk], functools.partial(one_pair, code_ref=code_ref), last)
    out_ref[...] = acc_ref[pl.ds(0, here)]
    wire_ref[...] = acc_ref[pl.ds(here, here)].astype(bf16)


def trip_kernel(dims, start, place_ref, facts_ref, own_ref, side_ref, lse_ref, *refs):
    groups = (len(refs) - 4) // 2
    plane = Plane(refs[:groups], dims)
    grad_refs, (query_ref, panel_ref, meta_ref, acc_ref) = refs[groups : 2 * groups], refs[2 * groups :]
    blocks = own_ref.shape[0] // BLOCK
    tb, trips = plane.tb, plane.trips
    plane.numbers(meta_ref)

    def before(t):
        plane.queries(query_ref, t)
        acc_ref[...] = jnp.zeros_like(acc_ref)

    def pair(t, k, block, length):
        load_panel(panel_ref, (own_ref, side_ref), block, blocks)
        picks = plane.chosen(meta_ref, t) - k * BLOCK
        lse = lse_ref[pl.ds(start + t, 1), :]

        def body(height):
            panel = panel_ref[pl.ds(0, height), :]
            weights = pair_weights(panel, query_ref[...], length, lse, picks)
            acc_ref[...] += lax.dot_general(panel, weights, (((0,), (0,)), ((), ())), preferred_element_type=f32)

        by_height(length, body)

    def after(t):
        grad = acc_ref[...].T.astype(bf16)
        for j, ref in enumerate(grad_refs):

            @pl.when((t >= j * tb) & (t < (j + 1) * tb))
            def _(j=j, ref=ref):
                ref[pl.ds(pl.multiple_of((t - j * tb) * trips, trips), trips), :] = grad

    visit(place_ref, facts_ref, blocks, plane, before, pair, after)


def kernel_call(body, smem, vmem, outs, out_specs, pairs, scratch, name):
    ins = list(smem) + list(vmem)
    moved = sum(x.size * x.dtype.itemsize for x in ins) + sum(o.size * o.dtype.itemsize for o in outs)
    return pl.pallas_call(
        body,
        out_shape=tuple(outs),
        in_specs=[SMEM] * len(smem) + [VMEM] * len(vmem),
        out_specs=tuple(out_specs),
        scratch_shapes=list(scratch),
        compiler_params=pltpu.CompilerParams(vmem_limit_bytes=48 * 1024 * 1024),
        cost_estimate=pl.CostEstimate(flops=pairs * (1 << 28), bytes_accessed=moved, transcendentals=pairs * (1 << 18)),
        name=name,
    )(*ins)


def swap(x, s):
    n = lax.axis_size("prod")
    return lax.ppermute(x, "prod", [(i, i ^ s) for i in range(n)])


def flip(x, s):
    n = x.shape[0]
    return jnp.flip(x.reshape((n // (2 * s), 2, s) + x.shape[1:]), axis=1).reshape(x.shape)


def tie(x, after):
    return lax.optimization_barrier((x,) + tuple(after))[0] if after else x


def struct(shape, dtype):
    return jax.ShapeDtypeStruct(shape, dtype)


def local(trip_vecs, table, consider, lengths, chosen):
    n = lax.axis_size("prod")
    me = lax.axis_index("prod").astype(i32)
    nz = lax.axis_size("trip")
    width = table.shape[1]
    blocks = table.shape[0] // BLOCK
    tb, per_block = consider.shape
    here = trip_vecs.shape[0]
    trips = here // tb
    dims = (tb, per_block, trips)
    per_chunk = blocks // CHUNKS
    chips = n // 2
    bits = [1 << j for j in range(chips.bit_length() - 1)]
    place = jnp.stack([(me - me % 2) * blocks, me % 2])

    meta = [jnp.pad(x, ((0, 0), (0, LANES - per_block))) for x in (consider, lengths)]
    meta = jnp.concatenate(meta + [chosen.reshape(-1, LANES)])
    lines = meta.shape[0]
    meta = jnp.concatenate([meta // DIGIT, meta % DIGIT]).astype(bf16)
    own = jnp.concatenate([trip_vecs, meta])
    side = swap(table, 1)
    sent = [own] + [swap(own, 2 * s) for s in range(1, chips)]

    def facts_of(group):
        both = jnp.stack([sent[s][here:] for s in group])
        hi, lo = both[:, : 2 * tb].astype(i32), both[:, lines : lines + 2 * tb].astype(i32)
        return (hi * DIGIT + lo)[:, :, :per_block]

    def scratch(group):
        return [
            pltpu.VMEM((trips, width), bf16),
            pltpu.VMEM((BLOCK, width), bf16),
            pltpu.VMEM((len(group) * lines, LANES), i32),
        ]

    cuts = [0, 1, chips - 1, chips] if chips > 2 else [0, chips]
    sums, picked, codes, counts, before = [], [], [], [], ()
    for lo, hi in zip(cuts[:-1], cuts[1:]):
        group = range(lo, hi)
        facts = facts_of(group)
        out = struct((len(group) * tb, trips), f32)
        row = pltpu.VMEM((1, trips), f32)
        got = kernel_call(
            functools.partial(lse_kernel, dims, lo * tb),
            [tie(place, before), facts],
            [table, side] + [sent[s] for s in group],
            [out, out, struct((CHUNKS, len(group) * tb * per_block), i32), struct((CHUNKS,), i32)],
            [VMEM] * 2 + [SMEM] * 2,
            len(group) * 2,
            scratch(group) + [row] * 3,
            "lse",
        )
        before = (got[0],)
        for to, x in zip((sums, picked, codes, counts), got):
            to.append(x)

    lse = jnp.concatenate(sums).reshape(chips, tb, trips)
    picked = jnp.concatenate(picked).reshape(chips, tb, trips)
    for s in bits:
        got = swap(jnp.concatenate([lse, picked[1::2]]), 2 * s)
        lse = jnp.logaddexp(lse, flip(got[:chips], s))
        picked = picked[0::2] + got[chips:]
    losses = (lse[0] - picked[0]).reshape(-1)
    lse = lse.reshape(chips * tb, trips)

    def table_part(c, after):
        out = (per_chunk, BLOCK, width)
        return kernel_call(
            functools.partial(table_kernel, dims, c, len(codes)),
            [tie(counts[0], after)] + counts[1:] + codes,
            [table, side, lse] + sent,
            [struct(out, f32), struct(out, bf16)],
            [VMEM] * 2,
            chips,
            scratch(sent) + [pltpu.VMEM((2 * per_chunk, BLOCK, width), f32)],
            "table_grad",
        )

    def trip_part(group, after):
        return kernel_call(
            functools.partial(trip_kernel, dims, group[0] * tb),
            [tie(place, after), facts_of(group)],
            [table, side, lse] + [sent[s] for s in group],
            [struct((here, width), bf16)] * len(group),
            [VMEM] * len(group),
            2 * len(group),
            scratch(group) + [pltpu.VMEM((width, trips), f32)],
            "trip_grad",
        )

    half = nz // 2
    at_z = lax.axis_index("trip")

    def pair_up(total, wire):
        total = total + swap(wire, 1).astype(f32)
        return total, total.astype(bf16)

    def inward(j, total, wire):
        got = lax.ppermute(wire, "trip", [(j, j + 1), (nz - 1 - j, nz - 2 - j)])
        total = total + got.astype(f32)
        return total, total.astype(bf16)

    def across(total, wire):
        got = lax.ppermute(wire, "trip", [(half - 1, half), (half, half - 1)])
        return total, (wire.astype(f32) + got.astype(f32)).astype(bf16)

    def outward(j, total, wire):
        got = lax.ppermute(wire, "trip", [(j + 1, j), (nz - 2 - j, nz - 1 - j)])
        return total, jnp.where((at_z == j) | (at_z == nz - 1 - j), got, wire)

    stages = [functools.partial(inward, j) for j in range(half - 1)]
    stages += [across] * (nz > 1)
    stages += [functools.partial(outward, j) for j in reversed(range(half - 1))]

    flight, finished = [], {}

    def advance():
        moved = []
        for c, stage, state in flight:
            if stage < len(stages):
                moved.append((c, stage + 1, stages[stage](*state)))
            else:
                finished[c] = state[1]
        flight[:] = moved

    table_grads = jnp.zeros((blocks, BLOCK, width), f32)
    after = ()
    for c in range(CHUNKS):
        got = table_part(c, after)
        advance()
        state = pair_up(*got)
        flight.append((c, 0, state))
        after = (got[1],) + tuple(state[1] for _, _, state in flight)
    grads = {}
    groups = [range(chips - 1, chips)] * (chips > 2) + [range(1, max(2, chips - 1)), range(1)]
    for group in groups:
        got = trip_part(list(group), after)
        grads.update(zip(group, got))
        advance()
        after = (got[0],) + tuple(state[1] for _, _, state in flight)
    while flight:
        advance()
    for c in range(CHUNKS):
        table_grads = lax.dynamic_update_slice(table_grads, finished[c].astype(f32), (c * per_chunk, 0, 0))

    total = grads[0].astype(f32)
    for s in range(1, chips):
        total = total + swap(grads[s], 2 * s).astype(f32)
    return losses, total, table_grads.reshape(-1, width)


def solution(mesh):
    return jax.shard_map(
        local,
        mesh=mesh,
        in_specs=(
            P(("prod", "trip"), None),
            P("prod", None),
            P(("prod", "trip"), None),
            P(("prod", "trip"), None),
            P(("prod", "trip")),
        ),
        out_specs=(P(("prod", "trip")), P(("prod", "trip"), None), P("prod", None)),
        check_vma=False,
    )
```
